512 devices in a mesh: ctx: 128 (over z, y, core), tp: 4 (over x).
Axes of the slice: x: 4, y: 4, z: 16, core: 2. Of those that a mesh axis runs over, the one named last changes fastest.
Arguments:
- short_query: bfloat16 [16384, 2048], P('ctx', 'tp'), may hold values from -6 to 6
- short_key: bfloat16 [16384, 2048], P('ctx', 'tp'), may hold values from -6 to 6
- short_value: bfloat16 [16384, 2048], P('ctx', 'tp'), may hold values from -6 to 6
- short_filter: bfloat16 [128, 2048], P(None, 'tp'), may hold values from -0.5 to 0.5
- long_query: bfloat16 [16384, 2048], P('ctx', 'tp'), may hold values from -6 to 6
- long_key: bfloat16 [16384, 2048], P('ctx', 'tp'), may hold values from -6 to 6
- long_filter: bfloat16 [16384, 2048], P('ctx', 'tp'), may hold values from -0.046875 to 0.046875
- out_weight: bfloat16 [2048, 2048], P('tp'), may hold values from -0.125 to 0.125
- out_grad: bfloat16 [16384, 2048], P('ctx', 'tp'), may hold values from -6 to 6
Outputs:
- short_query_grad: bfloat16 [16384, 2048], P('ctx', 'tp')
- short_key_grad: bfloat16 [16384, 2048], P('ctx', 'tp')
- short_value_grad: bfloat16 [16384, 2048], P('ctx', 'tp')
- short_filter_grad: bfloat16 [128, 2048], P(None, 'tp')
- long_query_grad: bfloat16 [16384, 2048], P('ctx', 'tp')
- long_key_grad: bfloat16 [16384, 2048], P('ctx', 'tp')
- long_filter_grad: bfloat16 [16384, 2048], P('ctx', 'tp')
The draws below stay inside these ranges and needn't reach their ends.
All inputs are finite; a program needn't handle non-finite values.
Results may differ from the reference program's by a relative error of at most 0.015.
Values may be sent and summed in bfloat16 or wider, within the bound.
No kernel may reach another device: no remote copies, remote signals or barrier semaphores. Data moves between devices by JAX's collectives and lax.ppermute only.
A program may use at most 64 MiB of HBM per device.

```python
import math
import jax
import jax.numpy as jnp
from jax import lax

D = 2048
TAPS = 128
SEQ = 16384


def level_of(key, dims, split, low, largest):
    gain = 1.0
    for position, shards_of in split:
        steps = jax.random.uniform(jax.random.fold_in(jax.random.fold_in(key, 6), position), (shards_of,), jnp.float32, low / len(split), largest / len(split))
        gain = gain * jnp.repeat(jnp.exp(steps), dims[position] // shards_of).reshape((-1,) + (1,) * (len(dims) - 1 - position))
    return gain


def normal_values(key, extent, spread, most, split=(), kind=jnp.bfloat16):
    drawn = spread * jax.random.normal(key, extent, jnp.float32)
    if split:
        drawn = drawn * level_of(key, extent, split, -0.22, 0.18)
    return jnp.clip(drawn, -most, most).astype(kind)


def setup_inputs(seed: int = 0) -> dict:
    seeds = jax.random.split(jax.random.key(seed), 10)
    return {
        "short_query": normal_values(seeds[0], (SEQ, D), 1.0, 6.0, ((0, 128), (1, 4))),
        "short_key": normal_values(seeds[1], (SEQ, D), 1.0, 6.0, ((0, 128), (1, 4))),
        "short_value": normal_values(seeds[2], (SEQ, D), 1.0, 6.0, ((0, 128), (1, 4))),
        "short_filter": normal_values(seeds[3], (TAPS, D), TAPS ** -0.5, 0.5, ((1, 4),)),
        "long_query": normal_values(seeds[4], (SEQ, D), 1.0, 6.0, ((0, 128), (1, 4))),
        "long_key": normal_values(seeds[5], (SEQ, D), 1.0, 6.0, ((0, 128), (1, 4))),
        "long_filter": normal_values(seeds[6], (SEQ, D), SEQ ** -0.5, 0.046875, ((0, 128), (1, 4))),
        "out_weight": normal_values(seeds[7], (D, D), D ** -0.5, 0.125, ((0, 4),)),
        "out_grad": normal_values(seeds[8], (SEQ, D), 1.0, 6.0, ((0, 128), (1, 4))),
    }


def causal_taps(values, weights):
    filter_taps = weights.shape[0]
    length = values.shape[0]
    padded = jnp.pad(values.astype(jnp.float32), ((filter_taps - 1, 0), (0, 0)))

    def add_tap(offset, total):
        place = jnp.asarray(offset).astype(jnp.int32)
        weight_row = lax.dynamic_index_in_dim(weights, place, 0, keepdims=False).astype(jnp.float32)
        shifted = lax.dynamic_slice_in_dim(padded, filter_taps - 1 - place, length, 0)
        return total + weight_row[None, :] * shifted
    return lax.fori_loop(0, filter_taps, add_tap, jnp.zeros(values.shape, jnp.float32))

def anti_taps(values, weights):
    filter_taps = weights.shape[0]
    length = values.shape[0]
    padded = jnp.pad(values.astype(jnp.float32), ((0, filter_taps - 1), (0, 0)))

    def add_tap(offset, total):
        place = jnp.asarray(offset).astype(jnp.int32)
        weight_row = lax.dynamic_index_in_dim(weights, place, 0, keepdims=False).astype(jnp.float32)
        shifted = lax.dynamic_slice_in_dim(padded, place, length, 0)
        return total + weight_row[None, :] * shifted
    return lax.fori_loop(0, filter_taps, add_tap, jnp.zeros(values.shape, jnp.float32))

def tap_products(grads, values, filter_taps):
    length = values.shape[0]
    padded = jnp.pad(values.astype(jnp.float32), ((filter_taps - 1, 0), (0, 0)))

    def one_tap(place):
        shifted = lax.dynamic_slice_in_dim(padded, filter_taps - 1 - place, length, 0)
        return lax.optimization_barrier(jnp.sum(grads * shifted, axis=0))
    return lax.map(one_tap, jnp.arange(filter_taps, dtype=jnp.int32))

def reference(short_query, short_key, short_value, short_filter, long_query, long_key, long_filter, out_weight, out_grad):
    product_one = (short_key.astype(jnp.float32) * short_value.astype(jnp.float32)).astype(jnp.bfloat16)
    short_mix = causal_taps(product_one, short_filter)
    mixed = (short_query.astype(jnp.float32) * short_mix).astype(jnp.bfloat16)
    product_two = (long_key.astype(jnp.float32) * mixed.astype(jnp.float32)).astype(jnp.bfloat16)
    grad_two = jnp.dot(out_grad, out_weight.T, preferred_element_type=jnp.float32).astype(jnp.bfloat16)
    gated_two = (grad_two.astype(jnp.float32) * long_query.astype(jnp.float32)).astype(jnp.bfloat16)
    points = 2 * SEQ
    spec_prod = jnp.fft.rfft(product_two.astype(jnp.float32), n=points, axis=0)
    spec_gated = jnp.fft.rfft(gated_two.astype(jnp.float32), n=points, axis=0)
    spec_filter = jnp.fft.rfft(long_filter.astype(jnp.float32), n=points, axis=0)
    long_mix = jnp.fft.irfft(spec_filter * spec_prod, n=points, axis=0)[:SEQ]
    back_two = jnp.fft.irfft(jnp.conj(spec_filter) * spec_gated, n=points, axis=0)[:SEQ]
    filter_two = jnp.fft.irfft(jnp.conj(spec_prod) * spec_gated, n=points, axis=0)[:SEQ]
    scaling = 1.0 / math.sqrt(SEQ)
    long_query_grad = (grad_two.astype(jnp.float32) * long_mix).astype(jnp.bfloat16)
    long_key_grad = (back_two * mixed.astype(jnp.float32)).astype(jnp.bfloat16)
    mixed_grad = (back_two * long_key.astype(jnp.float32)).astype(jnp.bfloat16)
    long_filter_grad = (filter_two * scaling).astype(jnp.bfloat16)
    gated_one = (mixed_grad.astype(jnp.float32) * short_query.astype(jnp.float32)).astype(jnp.bfloat16)
    short_query_grad = (mixed_grad.astype(jnp.float32) * short_mix).astype(jnp.bfloat16)
    back_one = anti_taps(gated_one, short_filter)
    short_key_grad = (back_one * short_value.astype(jnp.float32)).astype(jnp.bfloat16)
    short_value_grad = (back_one * short_key.astype(jnp.float32)).astype(jnp.bfloat16)
    filter_one = tap_products(gated_one.astype(jnp.float32), product_one, short_filter.shape[0])
    short_filter_grad = (filter_one * scaling).astype(jnp.bfloat16)
    return (short_query_grad, short_key_grad, short_value_grad, short_filter_grad, long_query_grad, long_key_grad, long_filter_grad)
```

```python
import math

import jax
import jax.numpy as jnp
import numpy as np
from jax import lax
from jax.experimental import pallas as pl
from jax.experimental.pallas import tpu as pltpu
from jax.sharding import Mesh
from jax.sharding import PartitionSpec as P

CTX = ("ctx_0", "ctx_1", "ctx_2")
F32 = jnp.float32
BF16 = jnp.bfloat16
L = 128


def params():
    return pltpu.CompilerParams(vmem_limit_bytes=48 * 1024 * 1024)


def nn(a, b):
    return lax.dot_general(a, b, (((1,), (0,)), ((), ())), preferred_element_type=F32)


def nt(a, b):
    return lax.dot_general(a, b, (((1,), (1,)), ((), ())), preferred_element_type=F32)


def tn(a, b):
    return lax.dot_general(a, b, (((0,), (0,)), ((), ())), preferred_element_type=F32)


def halves(x):
    high = x.astype(BF16)
    return high, (x - high.astype(F32)).astype(BF16)


def np_halves(x):
    high = np.asarray(x, np.float32).astype(BF16)
    low = np.asarray(x - high.astype(np.float64), np.float32).astype(BF16)
    return high, low


def tables():
    whole = 2 * L * L
    k = np.arange(L) + 0.5
    n = np.arange(L)
    first = 2.0 * np.pi * np.outer(k, n) / (2 * L)
    one = np.concatenate([np.cos(first), -np.sin(first)], axis=0)
    one_high, one_low = np_halves(one)
    forward = np.concatenate([one_high, one_low], axis=1)
    back_high, back_low = np_halves(one.T * (2.0 / whole))
    twist = 2.0 * np.pi * np.outer(k, n) / whole
    cos_twist = np.cos(twist).astype(np.float32)
    sin_twist = np.sin(twist).astype(np.float32)
    second = 2.0 * np.pi * (np.outer(n, n) % L) / L
    cos_two, sin_two = np.cos(second), np.sin(second)
    two = np.block([[cos_two, -sin_two], [sin_two, cos_two]])
    two_high, two_low = np_halves(two)
    return (forward, back_high, back_low, cos_twist, sin_twist, two_high, two_low)


def pre_kernel(grads, weight, lq, sq, prod, lk, lf, out, grad_two, rows):
    total = nt(grads[0], weight[:, 0:512])
    for part in range(1, 4):
        total += nt(grads[part], weight[:, 512 * part : 512 * (part + 1)])
    grad_low = total.astype(BF16)
    grad_two[...] = grad_low
    gated = grad_low.astype(F32) * lq[...].astype(F32)
    gate = lk[...].astype(F32) * sq[...].astype(F32)
    for place, value in enumerate((lf[...].astype(F32), prod[...].astype(F32), gate, gated)):
        for c in range(4):
            rows[pl.ds(4 * place + c, L, stride=16), :] = value[:, L * c : L * (c + 1)].T
    out[...] = rows[...].reshape(L, 16, L).astype(BF16)


def tap_loop(ext, taps, extended_rows, causal, finish):
    def chunk(index, carry):
        lanes = pl.ds(pl.multiple_of(index * L, L), L)
        total = jnp.zeros((L, L), F32)
        for shift in range(8):
            if causal:
                extended_rows[8:256, :] = ext[8 - shift : 256 - shift, lanes]
            else:
                extended_rows[0:248, :] = ext[shift : 248 + shift, lanes]
            for group in range(16):
                start = L - 8 * group if causal else 8 * group
                tap = 8 * group + shift
                total += taps[tap : tap + 1, lanes] * extended_rows[start : start + L, :]
        finish(lanes, total)
        return carry

    lax.fori_loop(0, 4, chunk, 0)


def mix_kernel(before, prod, taps_in, out, ext, taps, extended_rows):
    ext[0:L, :] = before[...].astype(F32)
    ext[L : 2 * L, :] = prod[...].astype(F32)
    taps[...] = taps_in[...].astype(F32)

    def finish(lanes, total):
        out[:, lanes] = total

    tap_loop(ext, taps, extended_rows, True, finish)


def last_kernel(gated, after, taps_in, sk, sv, key_out, value_out, ext, taps, extended_rows):
    ext[0:L, :] = gated[...].astype(F32)
    ext[L : 2 * L, :] = after[...].astype(F32)
    taps[...] = taps_in[...].astype(F32)

    def finish(lanes, total):
        key_out[:, lanes] = (total * sv[:, lanes].astype(F32)).astype(BF16)
        value_out[:, lanes] = (total * sk[:, lanes].astype(F32)).astype(BF16)

    tap_loop(ext, taps, extended_rows, False, finish)


def spectral_kernel(
    place, arrived, taps_in, forward, back_high, back_low, cos_ref, sin_ref, high_ref, low_ref,
    out, rows,
):
    rows[0:16, :] = jnp.zeros((16, L), F32)
    rows[16:, :] = arrived[...].astype(F32).reshape(16 * L, L)

    def array(a, c, back=0):
        return rows[pl.ds(16 * (1 - back) + 4 * a + c, L, stride=16), :]

    row_index = lax.broadcasted_iota(jnp.int32, (L, L), 0)
    lane_index = lax.broadcasted_iota(jnp.int32, (L, L), 1)
    chosen = (lax.broadcasted_iota(jnp.int32, (16, L), 1) == place[0]).astype(F32).astype(BF16)
    flip = (row_index + lane_index == L - 1).astype(F32).astype(BF16)
    prods, earlier, gates = [], [], []
    product_two = []
    for c in range(4):
        prods.append(array(1, c).astype(BF16))
        earlier.append(array(1, c, 1).astype(BF16))
        gates.append(array(2, c))
        taps = nt(chosen, taps_in[:, L * c : L * (c + 1)])[0:1, :]
        turned = pltpu.roll(jnp.broadcast_to(taps, (L, L)), 0, 1, stride=1, stride_axis=0)
        own = jnp.where(lane_index >= row_index, turned, 0.0).astype(BF16)
        other = jnp.where(lane_index < row_index, turned, 0.0).astype(BF16)
        short_mix = nn(prods[c], own) + nn(earlier[c], other)
        product_two.append((gates[c] * short_mix).astype(BF16))

    cos_t, sin_t = cos_ref[...], sin_ref[...]
    high, low = high_ref[...], low_ref[...]

    def spectrum(columns):
        both = jnp.concatenate(columns, axis=1)
        first = nn(forward[...], jnp.concatenate([both, both], axis=0))
        turned = []
        for c in range(4):
            real = first[0:L, L * c : L * (c + 1)]
            imag = first[L : 2 * L, L * c : L * (c + 1)]
            turned.append(
                jnp.concatenate(
                    [real * cos_t + imag * sin_t, imag * cos_t - real * sin_t], axis=1
                )
            )
        coarse, fine = halves(jnp.concatenate(turned, axis=0))
        result = nn(coarse, high) + nn(coarse, low) + nn(fine, high)
        return result[:, 0:L], result[:, L : 2 * L]

    def restore(real, imag):
        coarse, fine = halves(jnp.concatenate([real, imag], axis=1))
        turned = nt(coarse, high) + nt(coarse, low) + nt(fine, high)
        columns = []
        for c in range(4):
            real = turned[L * c : L * (c + 1), 0:L]
            imag = turned[L * c : L * (c + 1), L : 2 * L]
            columns.append(
                jnp.concatenate(
                    [real * cos_t - imag * sin_t, imag * cos_t + real * sin_t], axis=0
                )
            )
        coarse, fine = halves(jnp.concatenate(columns, axis=1))
        return nn(back_high[...], coarse) + nn(back_high[...], fine) + nn(back_low[...], coarse)

    real_h, imag_h = spectrum([array(0, c).astype(BF16) for c in range(4)])
    real_g, imag_g = spectrum([array(3, c).astype(BF16) for c in range(4)])
    real_u, imag_u = spectrum(product_two)
    back_two = restore(real_h * real_g + imag_h * imag_g, real_h * imag_g - imag_h * real_g)
    long_mix = restore(real_h * real_u - imag_h * imag_u, real_h * imag_u + imag_h * real_u)
    filter_two = restore(real_u * real_g + imag_u * imag_g, real_u * imag_g - imag_u * real_g)
    scaling = 1.0 / L
    for c in range(4):
        part = slice(L * c, L * (c + 1))
        gated_one = (back_two[:, part] * gates[c]).astype(BF16)
        now = tn(nn(prods[c], flip).astype(BF16), gated_one)
        then = tn(nn(earlier[c], flip).astype(BF16), gated_one)
        pairs = jnp.where(lane_index >= L - 1 - row_index, now, then)
        turned = pltpu.roll(pairs, 1, 1, stride=1, stride_axis=0)
        filter_one = jnp.sum(turned, axis=0, keepdims=True) * scaling
        rows[pl.ds(c, L, stride=16), :] = back_two[:, part]
        rows[pl.ds(4 + c, L, stride=16), :] = long_mix[:, part]
        rows[pl.ds(8 + c, L, stride=16), :] = filter_two[:, part] * scaling
        rows[pl.ds(12 + c, L, stride=16), :] = jnp.broadcast_to(filter_one, (L, L))
    out[...] = rows[0 : 16 * L, :].reshape(L, 16, L).astype(BF16)


def post_kernel(
    arrived, grad_two, short_mix, sq, lk, query_out, key_out, filter_out, taps_out, short_out,
    gated_out, rows,
):
    rows[...] = arrived[...].astype(F32).reshape(16 * L, L)

    def array(a, c):
        return rows[pl.ds(4 * a + c, L, stride=16), :].T

    for c in range(4):
        lanes = slice(L * c, L * (c + 1))
        back_two = array(0, c)
        mix = short_mix[:, lanes]
        query = sq[:, lanes].astype(F32)
        mixed = (query * mix).astype(BF16).astype(F32)
        mixed_grad = (back_two * lk[:, lanes].astype(F32)).astype(BF16).astype(F32)
        gated_out[:, lanes] = (mixed_grad * query).astype(BF16)
        short_out[:, lanes] = (mixed_grad * mix).astype(BF16)
        key_out[:, lanes] = (back_two * mixed).astype(BF16)
        query_out[:, lanes] = (grad_two[:, lanes].astype(F32) * array(1, c)).astype(BF16)
        filter_out[:, lanes] = array(2, c).astype(BF16)
        taps_out[:, lanes] = array(3, c).astype(BF16)


def passed_along(block, axis, distance):
    devices = range(lax.axis_size(axis))
    route = [(i - distance, i) for i in devices if i - distance in devices]
    return lax.ppermute(block, axis, route)


def body(sq, sk, sv, taps, lq, lk, lf, weight, out_grad):
    block = jax.ShapeDtypeStruct((L, 4 * L), BF16)
    payload = jax.ShapeDtypeStruct((L, 16, L), BF16)
    peers = lax.axis_size("tp")
    grads = lax.all_to_all(
        jnp.broadcast_to(out_grad[None], (peers, *out_grad.shape)), "tp", 0, 0, tiled=True
    )
    prod = (sk.astype(F32) * sv.astype(F32)).astype(BF16)
    before = passed_along(prod, CTX, 1)
    sent, grad_two = pl.pallas_call(
        pre_kernel,
        out_shape=(payload, block),
        scratch_shapes=[pltpu.VMEM((16 * L, L), F32)],
        compiler_params=params(),
        name="pre",
    )(grads, weight, lq, sq, prod, lk, lf)
    arrived = lax.all_to_all(sent, CTX, 0, 0, tiled=True)
    conv_scratch = [
        pltpu.VMEM((2 * L, 4 * L), F32), pltpu.VMEM((L, 4 * L), F32), pltpu.VMEM((2 * L, L), F32)
    ]
    short_mix = pl.pallas_call(
        mix_kernel,
        out_shape=jax.ShapeDtypeStruct((L, 4 * L), F32),
        scratch_shapes=conv_scratch,
        compiler_params=params(),
        name="mix",
    )(before, prod, taps)
    place = lax.axis_index(CTX).astype(jnp.int32).reshape(1)
    vmem = pl.BlockSpec(memory_space=pltpu.VMEM)
    returned = pl.pallas_call(
        spectral_kernel,
        out_shape=payload,
        in_specs=[pl.BlockSpec(memory_space=pltpu.SMEM)] + [vmem] * 9,
        scratch_shapes=[pltpu.VMEM((16 * L + 16, L), F32)],
        compiler_params=params(),
        name="spectral",
    )(place, arrived, taps, *(jnp.asarray(t) for t in tables()))
    landed = lax.all_to_all(returned, CTX, 0, 0, tiled=True)
    query_out, key_out, filter_out, taps_out, short_out, gated = pl.pallas_call(
        post_kernel,
        out_shape=(block,) * 6,
        scratch_shapes=[pltpu.VMEM((16 * L, L), F32)],
        compiler_params=params(),
        name="post",
    )(landed, grad_two, short_mix, sq, lk)
    after = passed_along(gated, CTX, -1)
    short_key_grad, short_value_grad = pl.pallas_call(
        last_kernel,
        out_shape=(block, block),
        scratch_shapes=conv_scratch,
        compiler_params=params(),
        name="last",
    )(gated, after, taps, sk, sv)
    return (
        short_out, short_key_grad, short_value_grad, taps_out, query_out, key_out, filter_out
    )


def solution(mesh):
    split = Mesh(
        mesh.devices.reshape(16, 4, 2, mesh.shape["tp"]), ("ctx_0", "ctx_1", "ctx_2", "tp")
    )
    rows = P(CTX, "tp")
    columns = P(None, "tp")
    return jax.shard_map(
        body,
        mesh=split,
        in_specs=(rows, rows, rows, columns, rows, rows, rows, P("tp", None), rows),
        out_specs=(rows, rows, rows, columns, rows, rows, rows),
        check_vma=False,
    )
```

```python
import jax
import jax.numpy as jnp
import numpy as np
from jax import lax
from jax.experimental import pallas as pl
from jax.experimental.pallas import tpu as pltpu
from jax.sharding import Mesh
from jax.sharding import PartitionSpec as P


CTX = ("ctx_0", "ctx_1", "ctx_2")
F32 = jnp.float32
BF16 = jnp.bfloat16
L = 128


def params():
    return pltpu.CompilerParams(vmem_limit_bytes=24 * 1024 * 1024)


def nn(a, b):
    return lax.dot_general(a, b, (((1,), (0,)), ((), ())), preferred_element_type=F32)


def nt(a, b):
    return lax.dot_general(a, b, (((1,), (1,)), ((), ())), preferred_element_type=F32)


def tn(a, b):
    return lax.dot_general(a, b, (((0,), (0,)), ((), ())), preferred_element_type=F32)


def halves(x):
    high = x.astype(BF16)
    return high, (x - high.astype(F32)).astype(BF16)


def np_halves(x):
    high = np.asarray(x, np.float32).astype(BF16)
    low = np.asarray(x - high.astype(np.float64), np.float32).astype(BF16)
    return high, low


def tables():
    whole = 2 * L * L
    k = np.arange(L) + 0.5
    n = np.arange(L)
    first = 2.0 * np.pi * np.outer(k, n) / (2 * L)
    one = np.concatenate([np.cos(first), -np.sin(first)], axis=0)
    one_high, one_low = np_halves(one)
    forward = np.concatenate([one_high, one_low], axis=1)
    back_high, back_low = np_halves(one.T * (2.0 / whole))
    twist = 2.0 * np.pi * np.outer(k, n) / whole
    cos_twist = np.cos(twist).astype(np.float32)
    sin_twist = np.sin(twist).astype(np.float32)
    second = 2.0 * np.pi * (np.outer(n, n) % L) / L
    cos_two, sin_two = np.cos(second), np.sin(second)
    two = np.block([[cos_two, -sin_two], [sin_two, cos_two]])
    two_high, two_low = np_halves(two)
    return (forward, two_high, two_low, cos_twist, sin_twist, back_high, back_low)


def far(array):
    return pltpu.with_memory_space_constraint(array, pltpu.HBM)


def fetch(sources, targets, marks):
    copies = [
        pltpu.make_async_copy(source, target, marks.at[k])
        for k, (source, target) in enumerate(zip(sources, targets))
    ]
    for copy in copies:
        copy.start()
    return copies


def put(rows, place, value):
    for c in range(4):
        rows[pl.ds(4 * place + c, L, stride=16), :] = value[:, L * c : L * (c + 1)].T


def spread_kernel(grads, out, grads_v, marks_in, marks_out):
    parts = [pl.ds(L // 2 * half, L // 2) for half in range(2)]
    copies = fetch(
        [grads.at[part, :] for part in parts], [grads_v.at[part, :] for part in parts], marks_in
    )
    outward = []
    for half, part in enumerate(parts):
        copies[half].wait()
        outward += fetch(
            [grads_v.at[part, :]] * 4, [out.at[k, part, :] for k in range(4)], marks_out.at[half]
        )
    for copy in outward:
        copy.wait()


def stage_kernel(
    lf, sk, sv, lk, sq, weight, out, gate, prod, weight_v, rows, out_v, lf_v, sk_v, sv_v, lk_v,
    sq_v, marks,
):
    copies = fetch((lf, sk, sv, lk, sq, weight), (lf_v, sk_v, sv_v, lk_v, sq_v, weight_v), marks)
    put(rows, 3, jnp.zeros((L, 4 * L), F32))
    copies[0].wait()
    put(rows, 0, lf_v[...].astype(F32))
    copies[1].wait()
    copies[2].wait()
    product = (sk_v[...].astype(F32) * sv_v[...].astype(F32)).astype(BF16)
    prod[...] = product
    put(rows, 1, product.astype(F32))
    copies[3].wait()
    copies[4].wait()
    put(rows, 2, lk_v[...].astype(F32) * sq_v[...].astype(F32))
    out_v[...] = rows[...].reshape(L, 16, L).astype(BF16)
    gate[...] = out_v[:, 8:16, :]
    copy = pltpu.make_async_copy(out_v, out, marks.at[6])
    copy.start()
    copies[5].wait()
    copy.wait()


def join_kernel(grads, gate, weight, lq, staged, out, grad_two, rows, lq_v, out_v, marks):
    copies = fetch([lq], [lq_v], marks)
    rows[...] = gate[...].astype(F32).reshape(8 * L, L)
    total = nt(grads[0], weight[:, 0:512])
    for part in range(1, 4):
        total += nt(grads[part], weight[:, 512 * part : 512 * (part + 1)])
    grad_low = total.astype(BF16)
    grad_two[...] = grad_low
    copies[0].wait()
    gated = grad_low.astype(F32) * lq_v[...].astype(F32)
    for c in range(4):
        rows[pl.ds(4 + c, L, stride=8), :] = gated[:, L * c : L * (c + 1)].T
    out_v[...] = rows[...].reshape(L, 8, L).astype(BF16)
    copy = pltpu.make_async_copy(out_v, out.at[:, 8:16, :], marks.at[1])
    copy.start()
    copy.wait()


def mix_loop(ext, taps, shifted, finish):
    def chunk(index, carry):
        lanes = pl.ds(pl.multiple_of(index * L, L), L)
        total = jnp.zeros((L, L), F32)
        for shift in range(8):
            shifted[8:256, :] = ext[8 - shift : 256 - shift, lanes]
            for group in range(16):
                start = L - 8 * group
                tap = 8 * group + shift
                total += taps[tap : tap + 1, lanes] * shifted[start : start + L, :]
        finish(lanes, total)
        return carry

    lax.fori_loop(0, 4, chunk, 0)


def mix_kernel(before, prod, taps_in, out, ext, taps, shifted):
    ext[0:L, :] = before[...].astype(F32)
    ext[L : 2 * L, :] = prod[...].astype(F32)
    taps[...] = taps_in[...].astype(F32)

    def finish(lanes, total):
        out[:, lanes] = total

    mix_loop(ext, taps, shifted, finish)


def back_loop(ext, taps, shifted, inside, finish):
    def chunk(index, carry):
        lanes = pl.ds(pl.multiple_of(index * L, L), L)
        total = [jnp.zeros((8, L), F32) for _ in range(16)]
        for shift in range(8):
            shifted[...] = ext[shift : L + shift, lanes]
            for group in range(16):
                tap = taps[8 * group + shift : 8 * group + shift + 1, lanes]
                for tile in range(16 - group if inside else group + 1):
                    source = tile + group if inside else tile
                    place = tile if inside else 15 - group + tile
                    total[place] += tap * shifted[8 * source : 8 * (source + 1), :]
        finish(lanes, jnp.concatenate(total, axis=0), index)
        return carry

    lax.fori_loop(0, 4, chunk, 0)


def last_kernel(after, partial, taps_in, sk, sv, key_out, value_out, ext, taps, shifted, key_v, value_v, marks):
    ext[0:8, :] = jnp.zeros((8, 4 * L), F32)
    ext[8:, :] = after[...].astype(F32)
    taps[...] = taps_in[...].astype(F32)

    def outward(lanes, index):
        return (
            pltpu.make_async_copy(key_v.at[:, lanes], key_out.at[:, lanes], marks.at[0, index]),
            pltpu.make_async_copy(value_v.at[:, lanes], value_out.at[:, lanes], marks.at[1, index]),
        )

    def finish(lanes, total, index):
        total += partial[:, lanes]
        key_v[:, lanes] = (total * sv[:, lanes].astype(F32)).astype(BF16)
        value_v[:, lanes] = (total * sk[:, lanes].astype(F32)).astype(BF16)
        for copy in outward(lanes, index):
            copy.start()

    back_loop(ext, taps, shifted, False, finish)
    for index in range(4):
        for copy in outward(pl.ds(L * index, L), index):
            copy.wait()


def load_kernel(*refs):
    count = len(refs) // 2
    for copy in fetch(refs[:count], refs[count : 2 * count], refs[-1]):
        copy.wait()


def spectral_kernel(
    place, arrived, taps_in, forward, high_ref, low_ref, cos_ref, sin_ref, back_high, back_low,
    out, rows,
):
    rows[0:16, :] = jnp.zeros((16, L), F32)
    rows[16:, :] = arrived[...].astype(F32).reshape(16 * L, L)

    def array(a, c, back=0):
        return rows[pl.ds(16 * (1 - back) + 4 * a + c, L, stride=16), :]

    row_index = lax.broadcasted_iota(jnp.int32, (L, L), 0)
    lane_index = lax.broadcasted_iota(jnp.int32, (L, L), 1)
    chosen = (lax.broadcasted_iota(jnp.int32, (16, L), 1) == place[0]).astype(F32).astype(BF16)
    flip = (row_index + lane_index == L - 1).astype(F32).astype(BF16)
    prods, earlier, gates = [], [], []
    product_two = []
    for c in range(4):
        prods.append(array(1, c).astype(BF16))
        earlier.append(array(1, c, 1).astype(BF16))
        gates.append(array(2, c))
        taps = nt(chosen, taps_in[:, L * c : L * (c + 1)])[0:1, :]
        turned = pltpu.roll(jnp.broadcast_to(taps, (L, L)), 0, 1, stride=1, stride_axis=0)
        own = jnp.where(lane_index >= row_index, turned, 0.0).astype(BF16)
        other = jnp.where(lane_index < row_index, turned, 0.0).astype(BF16)
        short_mix = nn(prods[c], own) + nn(earlier[c], other)
        product_two.append((gates[c] * short_mix).astype(BF16))

    cos_t, sin_t = cos_ref[...], sin_ref[...]
    high, low = high_ref[...], low_ref[...]

    def spectrum(columns):
        both = jnp.concatenate(columns, axis=1)
        first = nn(forward[...], jnp.concatenate([both, both], axis=0))
        turned = []
        for c in range(4):
            real = first[0:L, L * c : L * (c + 1)]
            imag = first[L : 2 * L, L * c : L * (c + 1)]
            turned.append(
                jnp.concatenate(
                    [real * cos_t + imag * sin_t, imag * cos_t - real * sin_t], axis=1
                )
            )
        coarse, fine = halves(jnp.concatenate(turned, axis=0))
        result = nn(coarse, high) + nn(coarse, low) + nn(fine, high)
        return result[:, 0:L], result[:, L : 2 * L]

    def restore(real, imag):
        coarse, fine = halves(jnp.concatenate([real, imag], axis=1))
        turned = nt(coarse, high) + nt(coarse, low) + nt(fine, high)
        columns = []
        for c in range(4):
            real = turned[L * c : L * (c + 1), 0:L]
            imag = turned[L * c : L * (c + 1), L : 2 * L]
            columns.append(
                jnp.concatenate(
                    [real * cos_t - imag * sin_t, imag * cos_t + real * sin_t], axis=0
                )
            )
        coarse, fine = halves(jnp.concatenate(columns, axis=1))
        return nn(back_high[...], coarse) + nn(back_high[...], fine) + nn(back_low[...], coarse)

    real_h, imag_h = spectrum([array(0, c).astype(BF16) for c in range(4)])
    real_g, imag_g = spectrum([array(3, c).astype(BF16) for c in range(4)])
    real_u, imag_u = spectrum(product_two)
    back_two = restore(real_h * real_g + imag_h * imag_g, real_h * imag_g - imag_h * real_g)
    long_mix = restore(real_h * real_u - imag_h * imag_u, real_h * imag_u + imag_h * real_u)
    filter_two = restore(real_u * real_g + imag_u * imag_g, real_u * imag_g - imag_u * real_g)
    scaling = 1.0 / L
    for c in range(4):
        part = slice(L * c, L * (c + 1))
        gated_one = (back_two[:, part] * gates[c]).astype(BF16)
        now = tn(nn(prods[c], flip).astype(BF16), gated_one)
        then = tn(nn(earlier[c], flip).astype(BF16), gated_one)
        pairs = jnp.where(lane_index >= L - 1 - row_index, now, then)
        turned = pltpu.roll(pairs, 1, 1, stride=1, stride_axis=0)
        filter_one = jnp.sum(turned, axis=0, keepdims=True) * scaling
        rows[pl.ds(c, L, stride=16), :] = back_two[:, part]
        rows[pl.ds(4 + c, L, stride=16), :] = long_mix[:, part]
        rows[pl.ds(8 + c, L, stride=16), :] = filter_two[:, part] * scaling
        rows[pl.ds(12 + c, L, stride=16), :] = jnp.broadcast_to(filter_one, (L, L))
    out[...] = rows[0 : 16 * L, :].reshape(L, 16, L).astype(BF16)


def turn_kernel(arrived, sq, lk, back_out, gated_out, rows):
    rows[...] = arrived[...].astype(F32).reshape(16 * L, L)
    for c in range(4):
        lanes = slice(L * c, L * (c + 1))
        back_two = rows[pl.ds(c, L, stride=16), :].T
        back_out[:, lanes] = back_two.astype(BF16)
        mixed_grad = (back_two * lk[:, lanes].astype(F32)).astype(BF16).astype(F32)
        gated_out[:, lanes] = (mixed_grad * sq[:, lanes].astype(F32)).astype(BF16)


def post_kernel(
    arrived, back, gated, grad_two, short_mix, sq, lk, taps_in, query_out, key_out, filter_out,
    taps_out, short_out, partial, rows, ext, taps, shifted, query_v, key_v, filter_v, taps_v,
    short_v, marks,
):
    rows[...] = arrived[...].astype(F32).reshape(16 * L, L)

    def array(a, c):
        return rows[pl.ds(4 * a + c, L, stride=16), :].T

    for c in range(4):
        lanes = slice(L * c, L * (c + 1))
        back_two = back[:, lanes].astype(F32)
        mix = short_mix[:, lanes]
        mixed = (sq[:, lanes].astype(F32) * mix).astype(BF16).astype(F32)
        mixed_grad = (back_two * lk[:, lanes].astype(F32)).astype(BF16).astype(F32)
        short_v[:, lanes] = (mixed_grad * mix).astype(BF16)
        key_v[:, lanes] = (back_two * mixed).astype(BF16)
        query_v[:, lanes] = (grad_two[:, lanes].astype(F32) * array(1, c)).astype(BF16)
        filter_v[:, lanes] = array(2, c).astype(BF16)
        taps_v[:, lanes] = array(3, c).astype(BF16)
    copies = fetch(
        (query_v, key_v, filter_v, taps_v, short_v),
        (query_out, key_out, filter_out, taps_out, short_out),
        marks,
    )
    ext[0:L, :] = gated[...].astype(F32)
    ext[L:, :] = jnp.zeros((8, 4 * L), F32)
    taps[...] = taps_in[...].astype(F32)

    def finish(lanes, total, index):
        partial[:, lanes] = total

    back_loop(ext, taps, shifted, True, finish)
    for copy in copies:
        copy.wait()


def passed_along(block, axis, distance):
    devices = range(lax.axis_size(axis))
    route = [(i - distance, i) for i in devices if i - distance in devices]
    return lax.ppermute(block, axis, route)


def body(sq, sk, sv, taps, lq, lk, lf, weight, out_grad):
    block = jax.ShapeDtypeStruct((L, 4 * L), BF16)
    payload = jax.ShapeDtypeStruct((L, 16, L), BF16)
    vmem = pl.BlockSpec(memory_space=pltpu.VMEM)
    smem = pl.BlockSpec(memory_space=pltpu.SMEM)
    hbm = pl.BlockSpec(memory_space=pltpu.HBM)
    tile = pltpu.VMEM((L, 4 * L), BF16)
    spread = pl.pallas_call(
        spread_kernel,
        out_shape=pltpu.HBM((4, L, 4 * L), BF16),
        in_specs=[hbm],
        out_specs=hbm,
        scratch_shapes=[tile, pltpu.SemaphoreType.DMA((2,)), pltpu.SemaphoreType.DMA((2, 4))],
        compiler_params=params(),
        name="spread",
    )(far(out_grad))
    grads = lax.all_to_all(spread, "tp", 0, 0, tiled=True)
    sent_shape = pltpu.HBM((L, 16, L), BF16)
    half = jax.ShapeDtypeStruct((L, 8, L), BF16)
    staged, gate, prod, weight_v = pl.pallas_call(
        stage_kernel,
        out_shape=(sent_shape, half, block, jax.ShapeDtypeStruct((4 * L, 16 * L), BF16)),
        in_specs=[hbm] * 6,
        out_specs=(hbm, vmem, vmem, vmem),
        scratch_shapes=[pltpu.VMEM((16 * L, L), F32), pltpu.VMEM((L, 16, L), BF16)]
        + [tile] * 5
        + [pltpu.SemaphoreType.DMA((7,))],
        compiler_params=params(),
        name="stage",
    )(*map(far, (lf, sk, sv, lk, sq, weight)))
    before = passed_along(prod, CTX, 1)
    sent, grad_two = pl.pallas_call(
        join_kernel,
        out_shape=(sent_shape, block),
        in_specs=[vmem, vmem, vmem, hbm, hbm],
        out_specs=(hbm, vmem),
        input_output_aliases={4: 0},
        scratch_shapes=[
            pltpu.VMEM((8 * L, L), F32), tile, pltpu.VMEM((L, 8, L), BF16),
            pltpu.SemaphoreType.DMA((2,)),
        ],
        compiler_params=params(),
        name="join",
    )(grads, gate, weight_v, far(lq), staged)
    arrived = lax.all_to_all(sent, CTX, 0, 0, tiled=True)
    constants = [jnp.asarray(t) for t in tables()]
    loaded = pl.pallas_call(
        load_kernel,
        out_shape=tuple(jax.ShapeDtypeStruct(t.shape, t.dtype) for t in constants),
        in_specs=[hbm] * 7,
        out_specs=(vmem,) * 7,
        scratch_shapes=[pltpu.SemaphoreType.DMA((7,))],
        compiler_params=params(),
        name="load",
    )(*map(far, constants))
    conv_scratch = [
        pltpu.VMEM((2 * L, 4 * L), F32), pltpu.VMEM((L, 4 * L), F32), pltpu.VMEM((2 * L, L), F32)
    ]
    short_mix = pl.pallas_call(
        mix_kernel,
        out_shape=jax.ShapeDtypeStruct((L, 4 * L), F32),
        scratch_shapes=conv_scratch,
        compiler_params=params(),
        name="mix",
    )(before, prod, taps)
    place = lax.axis_index(CTX).astype(jnp.int32).reshape(1)
    returned = pl.pallas_call(
        spectral_kernel,
        out_shape=payload,
        in_specs=[smem] + [vmem] * 9,
        scratch_shapes=[pltpu.VMEM((16 * L + 16, L), F32)],
        compiler_params=params(),
        name="spectral",
    )(place, arrived, taps, *loaded)
    landed = lax.all_to_all(returned, CTX, 0, 0, tiled=True)
    landed_rows = pltpu.VMEM((16 * L, L), F32)
    back, gated = pl.pallas_call(
        turn_kernel,
        out_shape=(block, block),
        scratch_shapes=[landed_rows],
        compiler_params=params(),
        name="turn",
    )(landed, sq, lk)
    after = passed_along(gated, CTX, -1)
    back_scratch = [
        pltpu.VMEM((L + 8, 4 * L), F32), pltpu.VMEM((L, 4 * L), F32), pltpu.VMEM((L, L), F32)
    ]
    out_block = pltpu.HBM((L, 4 * L), BF16)
    query_out, key_out, filter_out, taps_out, short_out, partial = pl.pallas_call(
        post_kernel,
        out_shape=(out_block,) * 5 + (jax.ShapeDtypeStruct((L, 4 * L), F32),),
        out_specs=(hbm,) * 5 + (vmem,),
        scratch_shapes=[landed_rows] + back_scratch + [tile] * 5 + [pltpu.SemaphoreType.DMA((5,))],
        compiler_params=params(),
        name="post",
    )(landed, back, gated, grad_two, short_mix, sq, lk, taps)
    short_key_grad, short_value_grad = pl.pallas_call(
        last_kernel,
        out_shape=(out_block,) * 2,
        out_specs=(hbm,) * 2,
        scratch_shapes=back_scratch + [tile] * 2 + [pltpu.SemaphoreType.DMA((2, 4))],
        compiler_params=params(),
        name="last",
    )(after, partial, taps, sk, sv)
    return (
        short_out, short_key_grad, short_value_grad, taps_out, query_out, key_out, filter_out
    )


def solution(mesh):
    split = Mesh(
        mesh.devices.reshape(16, 4, 2, mesh.shape["tp"]), ("ctx_0", "ctx_1", "ctx_2", "tp")
    )
    rows = P(CTX, "tp")
    columns = P(None, "tp")
    return jax.shard_map(
        body,
        mesh=split,
        in_specs=(rows, rows, rows, columns, rows, rows, rows, P("tp", None), rows),
        out_specs=(rows, rows, rows, columns, rows, rows, rows),
        check_vma=False,
    )
```

```python
import jax
import jax.numpy as jnp
import numpy as np
from jax import lax
from jax.experimental import pallas as pl
from jax.experimental.pallas import tpu as pltpu
from jax.sharding import Mesh
from jax.sharding import PartitionSpec as P


CTX = ("ctx_0", "ctx_1", "ctx_2")
F32 = jnp.float32
BF16 = jnp.bfloat16
L = 128


def params():
    return pltpu.CompilerParams(vmem_limit_bytes=24 * 1024 * 1024)


def nn(a, b):
    return lax.dot_general(a, b, (((1,), (0,)), ((), ())), preferred_element_type=F32)


def nt(a, b):
    return lax.dot_general(a, b, (((1,), (1,)), ((), ())), preferred_element_type=F32)


def tn(a, b):
    return lax.dot_general(a, b, (((0,), (0,)), ((), ())), preferred_element_type=F32)


def halves(x):
    high = x.astype(BF16)
    return high, (x - high.astype(F32)).astype(BF16)


def np_halves(x):
    high = np.asarray(x, np.float32).astype(BF16)
    low = np.asarray(x - high.astype(np.float64), np.float32).astype(BF16)
    return high, low


def tables():
    whole = 2 * L * L
    k = np.arange(L) + 0.5
    n = np.arange(L)
    first = 2.0 * np.pi * np.outer(k, n) / (2 * L)
    one = np.concatenate([np.cos(first), -np.sin(first)], axis=0)
    one_high, one_low = np_halves(one)
    forward = np.concatenate([one_high, one_low], axis=1)
    back_high, back_low = np_halves(one.T * (2.0 / whole))
    twist = 2.0 * np.pi * np.outer(k, n) / whole
    cos_twist = np.cos(twist).astype(np.float32)
    sin_twist = np.sin(twist).astype(np.float32)
    second = 2.0 * np.pi * (np.outer(n, n) % L) / L
    cos_two, sin_two = np.cos(second), np.sin(second)
    two = np.block([[cos_two, -sin_two], [sin_two, cos_two]])
    two_high, two_low = np_halves(two)
    return (forward, two_high, two_low, cos_twist, sin_twist, back_high, back_low)


def far(array):
    return pltpu.with_memory_space_constraint(array, pltpu.HBM)


def fetch(sources, targets, marks):
    copies = [
        pltpu.make_async_copy(source, target, marks.at[k])
        for k, (source, target) in enumerate(zip(sources, targets))
    ]
    for copy in copies:
        copy.start()
    return copies


def put(rows, place, value):
    for c in range(4):
        rows[pl.ds(4 * place + c, L, stride=16), :] = value[:, L * c : L * (c + 1)].T


def spread_kernel(grads, out, grads_v, marks_in, marks_out):
    parts = [pl.ds(L // 2 * half, L // 2) for half in range(2)]
    copies = fetch(
        [grads.at[part, :] for part in parts], [grads_v.at[part, :] for part in parts], marks_in
    )
    outward = []
    for half, part in enumerate(parts):
        copies[half].wait()
        outward += fetch(
            [grads_v.at[part, :]] * 4, [out.at[k, part, :] for k in range(4)], marks_out.at[half]
        )
    for copy in outward:
        copy.wait()


def stage_kernel(
    lf, sk, sv, lk, sq, lq, weight, out, gate, prod, turned_lq, weight_v, rows, out_v, lf_v, sk_v,
    sv_v, lk_v, sq_v, lq_v, marks,
):
    copies = fetch(
        (lf, sk, sv, lk, sq, lq, weight), (lf_v, sk_v, sv_v, lk_v, sq_v, lq_v, weight_v), marks
    )
    put(rows, 3, jnp.zeros((L, 4 * L), F32))
    copies[0].wait()
    put(rows, 0, lf_v[...].astype(F32))
    copies[1].wait()
    copies[2].wait()
    product = (sk_v[...].astype(F32) * sv_v[...].astype(F32)).astype(BF16)
    prod[...] = product
    put(rows, 1, product.astype(F32))
    copies[3].wait()
    copies[4].wait()
    put(rows, 2, lk_v[...].astype(F32) * sq_v[...].astype(F32))
    out_v[...] = rows[...].reshape(L, 16, L).astype(BF16)
    gate[...] = out_v[:, 8:16, :]
    copy = pltpu.make_async_copy(out_v, out, marks.at[7])
    copy.start()
    copies[5].wait()
    turned_lq[...] = lq_v[...].astype(F32).T.astype(BF16)
    copies[6].wait()
    copy.wait()


def join_kernel(grads, gate, weight, turned_lq, staged, out, grad_two, rows, out_v, mark):
    rows[...] = gate[...].astype(F32).reshape(8 * L, L)
    total = nt(weight[:, 0:512], grads[0])
    for part in range(1, 4):
        total += nt(weight[:, 512 * part : 512 * (part + 1)], grads[part])
    grad_low = total.astype(BF16)
    grad_two[...] = grad_low
    gated = grad_low.astype(F32) * turned_lq[...].astype(F32)
    for c in range(4):
        rows[pl.ds(4 + c, L, stride=8), :] = gated[L * c : L * (c + 1), :]
    out_v[...] = rows[...].reshape(L, 8, L).astype(BF16)
    copy = pltpu.make_async_copy(out_v, out.at[:, 8:16, :], mark)
    copy.start()
    copy.wait()


def mix_loop(ext, taps, shifted, finish):
    def chunk(index, carry):
        lanes = pl.ds(pl.multiple_of(index * L, L), L)
        total = jnp.zeros((L, L), F32)
        for shift in range(8):
            shifted[8:256, :] = ext[8 - shift : 256 - shift, lanes]
            for group in range(16):
                start = L - 8 * group
                tap = 8 * group + shift
                total += taps[tap : tap + 1, lanes] * shifted[start : start + L, :]
        finish(lanes, total)
        return carry

    lax.fori_loop(0, 4, chunk, 0)


def mix_kernel(before, prod, taps_in, out, ext, taps, shifted):
    ext[0:L, :] = before[...].astype(F32)
    ext[L : 2 * L, :] = prod[...].astype(F32)
    taps[...] = taps_in[...].astype(F32)

    def finish(lanes, total):
        out[:, lanes] = total

    mix_loop(ext, taps, shifted, finish)


def back_loop(ext, taps, shifted, inside, finish):
    def chunk(index, carry):
        lanes = pl.ds(pl.multiple_of(index * L, L), L)
        total = [jnp.zeros((8, L), F32) for _ in range(16)]
        for shift in range(8):
            shifted[...] = ext[shift : L + shift, lanes]
            for group in range(16):
                tap = taps[8 * group + shift : 8 * group + shift + 1, lanes]
                for tile in range(16 - group if inside else group + 1):
                    source = tile + group if inside else tile
                    place = tile if inside else 15 - group + tile
                    total[place] += tap * shifted[8 * source : 8 * (source + 1), :]
        finish(lanes, jnp.concatenate(total, axis=0), index)
        return carry

    lax.fori_loop(0, 4, chunk, 0)


def last_kernel(after, partial, taps_in, sk, sv, key_out, value_out, ext, taps, shifted, key_v, value_v, marks):
    ext[0:8, :] = jnp.zeros((8, 4 * L), F32)
    ext[8:, :] = after[...].astype(F32)
    taps[...] = taps_in[...].astype(F32)

    def outward(lanes, index):
        return (
            pltpu.make_async_copy(key_v.at[:, lanes], key_out.at[:, lanes], marks.at[0, index]),
            pltpu.make_async_copy(value_v.at[:, lanes], value_out.at[:, lanes], marks.at[1, index]),
        )

    def finish(lanes, total, index):
        total += partial[:, lanes]
        key_v[:, lanes] = (total * sv[:, lanes].astype(F32)).astype(BF16)
        value_v[:, lanes] = (total * sk[:, lanes].astype(F32)).astype(BF16)
        for copy in outward(lanes, index):
            copy.start()

    back_loop(ext, taps, shifted, False, finish)
    for index in range(4):
        for copy in outward(pl.ds(L * index, L), index):
            copy.wait()


def load_kernel(*refs):
    count = len(refs) // 2
    for copy in fetch(refs[:count], refs[count : 2 * count], refs[-1]):
        copy.wait()


def spectral_kernel(
    place, arrived, taps_in, forward, high_ref, low_ref, cos_ref, sin_ref, back_high, back_low,
    out, rows, half, out_v, marks,
):
    rows[0:16, :] = jnp.zeros((16, L), F32)
    rows[16:, :] = arrived[...].astype(F32).reshape(16 * L, L)

    def array(a, c, back=0):
        return rows[pl.ds(16 * (1 - back) + 4 * a + c, L, stride=16), :]

    row_index = lax.broadcasted_iota(jnp.int32, (L, L), 0)
    lane_index = lax.broadcasted_iota(jnp.int32, (L, L), 1)
    chosen = (lax.broadcasted_iota(jnp.int32, (16, L), 1) == place[0]).astype(F32).astype(BF16)
    flip = (row_index + lane_index == L - 1).astype(F32).astype(BF16)
    prods, earlier, gates = [], [], []
    product_two = []
    for c in range(4):
        prods.append(array(1, c).astype(BF16))
        earlier.append(array(1, c, 1).astype(BF16))
        gates.append(array(2, c))
        taps = nt(chosen, taps_in[:, L * c : L * (c + 1)])[0:1, :]
        turned = pltpu.roll(jnp.broadcast_to(taps, (L, L)), 0, 1, stride=1, stride_axis=0)
        own = jnp.where(lane_index >= row_index, turned, 0.0).astype(BF16)
        other = jnp.where(lane_index < row_index, turned, 0.0).astype(BF16)
        short_mix = nn(prods[c], own) + nn(earlier[c], other)
        product_two.append((gates[c] * short_mix).astype(BF16))

    cos_t, sin_t = cos_ref[...], sin_ref[...]
    high, low = high_ref[...], low_ref[...]

    def spectrum(columns):
        both = jnp.concatenate(columns, axis=1)
        first = nn(forward[...], jnp.concatenate([both, both], axis=0))
        turned = []
        for c in range(4):
            real = first[0:L, L * c : L * (c + 1)]
            imag = first[L : 2 * L, L * c : L * (c + 1)]
            turned.append(
                jnp.concatenate(
                    [real * cos_t + imag * sin_t, imag * cos_t - real * sin_t], axis=1
                )
            )
        coarse, fine = halves(jnp.concatenate(turned, axis=0))
        result = nn(coarse, high) + nn(coarse, low) + nn(fine, high)
        return result[:, 0:L], result[:, L : 2 * L]

    def restore(real, imag):
        coarse, fine = halves(jnp.concatenate([real, imag], axis=1))
        turned = nt(coarse, high) + nt(coarse, low) + nt(fine, high)
        columns = []
        for c in range(4):
            real = turned[L * c : L * (c + 1), 0:L]
            imag = turned[L * c : L * (c + 1), L : 2 * L]
            columns.append(
                jnp.concatenate(
                    [real * cos_t - imag * sin_t, imag * cos_t + real * sin_t], axis=0
                )
            )
        coarse, fine = halves(jnp.concatenate(columns, axis=1))
        return nn(back_high[...], coarse) + nn(back_high[...], fine) + nn(back_low[...], coarse)

    real_h, imag_h = spectrum([array(0, c).astype(BF16) for c in range(4)])
    real_g, imag_g = spectrum([array(3, c).astype(BF16) for c in range(4)])
    real_u, imag_u = spectrum(product_two)

    def send(half, group, first, second):
        for c in range(4):
            part = slice(L * c, L * (c + 1))
            half[pl.ds(c, L, stride=8), :] = first[:, part]
            half[pl.ds(4 + c, L, stride=8), :] = second[:, part]
        out_v[group] = half[...].reshape(L, 8, L).astype(BF16)
        copy = pltpu.make_async_copy(
            out_v.at[group], out.at[:, 8 * group : 8 * (group + 1), :], marks.at[group]
        )
        copy.start()
        return copy

    scaling = 1.0 / L
    back_two = restore(real_h * real_g + imag_h * imag_g, real_h * imag_g - imag_h * real_g)
    filter_ones = []
    for c in range(4):
        part = slice(L * c, L * (c + 1))
        gated_one = (back_two[:, part] * gates[c]).astype(BF16)
        now = tn(nn(prods[c], flip).astype(BF16), gated_one)
        then = tn(nn(earlier[c], flip).astype(BF16), gated_one)
        pairs = jnp.where(lane_index >= L - 1 - row_index, now, then)
        turned = pltpu.roll(pairs, 1, 1, stride=1, stride_axis=0)
        filter_one = jnp.sum(turned, axis=0, keepdims=True) * scaling
        filter_ones.append(jnp.broadcast_to(filter_one, (L, L)))
    long_mix = restore(real_h * real_u - imag_h * imag_u, real_h * imag_u + imag_h * real_u)
    early = send(half.at[0], 0, back_two, long_mix)
    filter_two = restore(real_u * real_g + imag_u * imag_g, real_u * imag_g - imag_u * real_g)
    late = send(half.at[1], 1, filter_two * scaling, jnp.concatenate(filter_ones, axis=1))
    early.wait()
    late.wait()


def turn_kernel(arrived, sq, lk, back_out, gated_out, rows):
    rows[...] = arrived[...].astype(F32).reshape(16 * L, L)
    for c in range(4):
        lanes = slice(L * c, L * (c + 1))
        back_two = rows[pl.ds(c, L, stride=16), :].T
        back_out[:, lanes] = back_two.astype(BF16)
        mixed_grad = (back_two * lk[:, lanes].astype(F32)).astype(BF16).astype(F32)
        gated_out[:, lanes] = (mixed_grad * sq[:, lanes].astype(F32)).astype(BF16)


def post_kernel(
    arrived, back, gated, grad_two, short_mix, sq, lk, taps_in, query_out, key_out, filter_out,
    taps_out, short_out, partial, rows, ext, taps, shifted, query_v, key_v, filter_v, taps_v,
    short_v, marks,
):
    rows[...] = arrived[...].astype(F32).reshape(16 * L, L)

    def array(a, c):
        return rows[pl.ds(4 * a + c, L, stride=16), :].T

    for c in range(4):
        lanes = slice(L * c, L * (c + 1))
        back_two = back[:, lanes].astype(F32)
        mix = short_mix[:, lanes]
        mixed = (sq[:, lanes].astype(F32) * mix).astype(BF16).astype(F32)
        mixed_grad = (back_two * lk[:, lanes].astype(F32)).astype(BF16).astype(F32)
        short_v[:, lanes] = (mixed_grad * mix).astype(BF16)
        key_v[:, lanes] = (back_two * mixed).astype(BF16)
        query_v[:, lanes] = (grad_two[lanes, :].astype(F32).T * array(1, c)).astype(BF16)
        filter_v[:, lanes] = array(2, c).astype(BF16)
        taps_v[:, lanes] = array(3, c).astype(BF16)
    copies = fetch(
        (query_v, key_v, filter_v, taps_v, short_v),
        (query_out, key_out, filter_out, taps_out, short_out),
        marks,
    )
    ext[0:L, :] = gated[...].astype(F32)
    ext[L:, :] = jnp.zeros((8, 4 * L), F32)
    taps[...] = taps_in[...].astype(F32)

    def finish(lanes, total, index):
        partial[:, lanes] = total

    back_loop(ext, taps, shifted, True, finish)
    for copy in copies:
        copy.wait()


def passed_along(block, axis, distance):
    devices = range(lax.axis_size(axis))
    route = [(i - distance, i) for i in devices if i - distance in devices]
    return lax.ppermute(block, axis, route)


def body(sq, sk, sv, taps, lq, lk, lf, weight, out_grad):
    block = jax.ShapeDtypeStruct((L, 4 * L), BF16)
    vmem = pl.BlockSpec(memory_space=pltpu.VMEM)
    smem = pl.BlockSpec(memory_space=pltpu.SMEM)
    hbm = pl.BlockSpec(memory_space=pltpu.HBM)
    tile = pltpu.VMEM((L, 4 * L), BF16)
    spread = pl.pallas_call(
        spread_kernel,
        out_shape=pltpu.HBM((4, L, 4 * L), BF16),
        in_specs=[hbm],
        out_specs=hbm,
        scratch_shapes=[tile, pltpu.SemaphoreType.DMA((2,)), pltpu.SemaphoreType.DMA((2, 4))],
        compiler_params=params(),
        name="spread",
    )(far(out_grad))
    grads = lax.all_to_all(spread, "tp", 0, 0, tiled=True)
    sent_shape = pltpu.HBM((L, 16, L), BF16)
    half = jax.ShapeDtypeStruct((L, 8, L), BF16)
    turned = jax.ShapeDtypeStruct((4 * L, L), BF16)
    staged, gate, prod, turned_lq, weight_v = pl.pallas_call(
        stage_kernel,
        out_shape=(sent_shape, half, block, turned, jax.ShapeDtypeStruct((4 * L, 16 * L), BF16)),
        in_specs=[hbm] * 7,
        out_specs=(hbm, vmem, vmem, vmem, vmem),
        scratch_shapes=[pltpu.VMEM((16 * L, L), F32), pltpu.VMEM((L, 16, L), BF16)]
        + [tile] * 6
        + [pltpu.SemaphoreType.DMA((8,))],
        compiler_params=params(),
        name="stage",
    )(*map(far, (lf, sk, sv, lk, sq, lq, weight)))
    before = passed_along(prod, CTX, 1)
    sent, grad_two = pl.pallas_call(
        join_kernel,
        out_shape=(sent_shape, turned),
        in_specs=[vmem, vmem, vmem, vmem, hbm],
        out_specs=(hbm, vmem),
        input_output_aliases={4: 0},
        scratch_shapes=[
            pltpu.VMEM((8 * L, L), F32), pltpu.VMEM((L, 8, L), BF16), pltpu.SemaphoreType.DMA,
        ],
        compiler_params=params(),
        name="join",
    )(grads, gate, weight_v, turned_lq, staged)
    arrived = lax.all_to_all(sent, CTX, 0, 0, tiled=True)
    constants = [jnp.asarray(t) for t in tables()]
    loaded = pl.pallas_call(
        load_kernel,
        out_shape=tuple(jax.ShapeDtypeStruct(t.shape, t.dtype) for t in constants),
        in_specs=[hbm] * 7,
        out_specs=(vmem,) * 7,
        scratch_shapes=[pltpu.SemaphoreType.DMA((7,))],
        compiler_params=params(),
        name="load",
    )(*map(far, constants))
    conv_scratch = [
        pltpu.VMEM((2 * L, 4 * L), F32), pltpu.VMEM((L, 4 * L), F32), pltpu.VMEM((2 * L, L), F32)
    ]
    short_mix = pl.pallas_call(
        mix_kernel,
        out_shape=jax.ShapeDtypeStruct((L, 4 * L), F32),
        scratch_shapes=conv_scratch,
        compiler_params=params(),
        name="mix",
    )(before, prod, taps)
    place = lax.axis_index(CTX).astype(jnp.int32).reshape(1)
    returned = pl.pallas_call(
        spectral_kernel,
        out_shape=sent_shape,
        in_specs=[smem] + [vmem] * 9,
        out_specs=hbm,
        scratch_shapes=[
            pltpu.VMEM((16 * L + 16, L), F32), pltpu.VMEM((2, 8 * L, L), F32),
            pltpu.VMEM((2, L, 8, L), BF16), pltpu.SemaphoreType.DMA((2,)),
        ],
        compiler_params=params(),
        name="spectral",
    )(place, arrived, taps, *loaded)
    landed = lax.all_to_all(returned, CTX, 0, 0, tiled=True)
    landed_rows = pltpu.VMEM((16 * L, L), F32)
    back, gated = pl.pallas_call(
        turn_kernel,
        out_shape=(block, block),
        scratch_shapes=[landed_rows],
        compiler_params=params(),
        name="turn",
    )(landed, sq, lk)
    after = passed_along(gated, CTX, -1)
    back_scratch = [
        pltpu.VMEM((L + 8, 4 * L), F32), pltpu.VMEM((L, 4 * L), F32), pltpu.VMEM((L, L), F32)
    ]
    out_block = pltpu.HBM((L, 4 * L), BF16)
    query_out, key_out, filter_out, taps_out, short_out, partial = pl.pallas_call(
        post_kernel,
        out_shape=(out_block,) * 5 + (jax.ShapeDtypeStruct((L, 4 * L), F32),),
        out_specs=(hbm,) * 5 + (vmem,),
        scratch_shapes=[landed_rows] + back_scratch + [tile] * 5 + [pltpu.SemaphoreType.DMA((5,))],
        compiler_params=params(),
        name="post",
    )(landed, back, gated, grad_two, short_mix, sq, lk, taps)
    short_key_grad, short_value_grad = pl.pallas_call(
        last_kernel,
        out_shape=(out_block,) * 2,
        out_specs=(hbm,) * 2,
        scratch_shapes=back_scratch + [tile] * 2 + [pltpu.SemaphoreType.DMA((2, 4))],
        compiler_params=params(),
        name="last",
    )(after, partial, taps, sk, sv)
    return (
        short_out, short_key_grad, short_value_grad, taps_out, query_out, key_out, filter_out
    )


def solution(mesh):
    split = Mesh(
        mesh.devices.reshape(16, 4, 2, mesh.shape["tp"]), ("ctx_0", "ctx_1", "ctx_2", "tp")
    )
    rows = P(CTX, "tp")
    columns = P(None, "tp")
    return jax.shard_map(
        body,
        mesh=split,
        in_specs=(rows, rows, rows, columns, rows, rows, rows, P("tp", None), rows),
        out_specs=(rows, rows, rows, columns, rows, rows, rows),
        check_vma=False,
    )
```

```python
import jax
import jax.numpy as jnp
import numpy as np
from jax import lax
from jax.experimental import pallas as pl
from jax.experimental.pallas import tpu as pltpu
from jax.sharding import Mesh
from jax.sharding import PartitionSpec as P


CTX = ("ctx_0", "ctx_1", "ctx_2")
F32 = jnp.float32
BF16 = jnp.bfloat16
L = 128


def params():
    return pltpu.CompilerParams(vmem_limit_bytes=24 * 1024 * 1024)


def nn(a, b):
    return lax.dot_general(a, b, (((1,), (0,)), ((), ())), preferred_element_type=F32)


def nt(a, b):
    return lax.dot_general(a, b, (((1,), (1,)), ((), ())), preferred_element_type=F32)


def tn(a, b):
    return lax.dot_general(a, b, (((0,), (0,)), ((), ())), preferred_element_type=F32)


def halves(x):
    high = x.astype(BF16)
    return high, (x - high.astype(F32)).astype(BF16)


def np_halves(x):
    high = np.asarray(x, np.float32).astype(BF16)
    low = np.asarray(x - high.astype(np.float64), np.float32).astype(BF16)
    return high, low


def tables():
    whole = 2 * L * L
    k = np.arange(L) + 0.5
    n = np.arange(L)
    first = 2.0 * np.pi * np.outer(k, n) / (2 * L)
    one = np.concatenate([np.cos(first), -np.sin(first)], axis=0)
    one_high, one_low = np_halves(one)
    forward = np.concatenate([one_high, one_low], axis=1)
    back_high, back_low = np_halves(one.T * (2.0 / whole))
    twist = 2.0 * np.pi * np.outer(k, n) / whole
    cos_twist = np.cos(twist).astype(np.float32)
    sin_twist = np.sin(twist).astype(np.float32)
    second = 2.0 * np.pi * (np.outer(n, n) % L) / L
    cos_two, sin_two = np.cos(second), np.sin(second)
    two = np.block([[cos_two, -sin_two], [sin_two, cos_two]])
    two_high, two_low = np_halves(two)
    return (forward, two_high, two_low, cos_twist, sin_twist, back_high, back_low)


def far(array):
    return pltpu.with_memory_space_constraint(array, pltpu.HBM)


def fetch(sources, targets, marks):
    copies = [
        pltpu.make_async_copy(source, target, marks.at[k])
        for k, (source, target) in enumerate(zip(sources, targets))
    ]
    for copy in copies:
        copy.start()
    return copies


def put(rows, place, value):
    for c in range(4):
        rows[pl.ds(4 * place + c, L, stride=16), :] = value[:, L * c : L * (c + 1)].T


def spread_kernel(grads, out, grads_v, marks_in, marks_out):
    parts = [pl.ds(L // 2 * half, L // 2) for half in range(2)]
    copies = fetch(
        [grads.at[part, :] for part in parts], [grads_v.at[part, :] for part in parts], marks_in
    )
    outward = []
    for half, part in enumerate(parts):
        copies[half].wait()
        outward += fetch(
            [grads_v.at[part, :]] * 4, [out.at[k, part, :] for k in range(4)], marks_out.at[half]
        )
    for copy in outward:
        copy.wait()


def stage_kernel(
    lf, sk, sv, lk, sq, lq, weight, out, gate, prod, turned_lq, weight_v, rows, out_v, lf_v, sk_v,
    sv_v, lk_v, sq_v, lq_v, marks,
):
    copies = fetch(
        (lf, sk, sv, lk, sq, lq, weight), (lf_v, sk_v, sv_v, lk_v, sq_v, lq_v, weight_v), marks
    )
    put(rows, 3, jnp.zeros((L, 4 * L), F32))
    copies[0].wait()
    put(rows, 0, lf_v[...].astype(F32))
    copies[1].wait()
    copies[2].wait()
    product = (sk_v[...].astype(F32) * sv_v[...].astype(F32)).astype(BF16)
    prod[...] = product
    put(rows, 1, product.astype(F32))
    copies[3].wait()
    copies[4].wait()
    put(rows, 2, lk_v[...].astype(F32) * sq_v[...].astype(F32))
    out_v[...] = rows[...].reshape(L, 16, L).astype(BF16)
    gate[...] = out_v[:, 8:16, :]
    copy = pltpu.make_async_copy(out_v, out, marks.at[7])
    copy.start()
    copies[5].wait()
    turned_lq[...] = lq_v[...].astype(F32).T.astype(BF16)
    copies[6].wait()
    copy.wait()


def join_kernel(grads, gate, weight, turned_lq, staged, out, grad_two, rows, out_v, mark):
    rows[...] = gate[...].astype(F32).reshape(8 * L, L)
    total = nt(weight[:, 0:512], grads[0])
    for part in range(1, 4):
        total += nt(weight[:, 512 * part : 512 * (part + 1)], grads[part])
    grad_low = total.astype(BF16)
    grad_two[...] = grad_low
    gated = grad_low.astype(F32) * turned_lq[...].astype(F32)
    for c in range(4):
        rows[pl.ds(4 + c, L, stride=8), :] = gated[L * c : L * (c + 1), :]
    out_v[...] = rows[...].reshape(L, 8, L).astype(BF16)
    copy = pltpu.make_async_copy(out_v, out.at[:, 8:16, :], mark)
    copy.start()
    copy.wait()


def mix_loop(ext, taps, shifted, finish):
    def chunk(index, carry):
        lanes = pl.ds(pl.multiple_of(index * L, L), L)
        total = jnp.zeros((L, L), F32)
        for shift in range(8):
            shifted[8:256, :] = ext[8 - shift : 256 - shift, lanes]
            for group in range(16):
                start = L - 8 * group
                tap = 8 * group + shift
                total += taps[tap : tap + 1, lanes] * shifted[start : start + L, :]
        finish(lanes, total)
        return carry

    lax.fori_loop(0, 4, chunk, 0)


def mix_kernel(before, prod, taps_in, out, ext, taps, shifted):
    ext[0:L, :] = before[...].astype(F32)
    ext[L : 2 * L, :] = prod[...].astype(F32)
    taps[...] = taps_in[...].astype(F32)

    def finish(lanes, total):
        out[:, lanes] = total

    mix_loop(ext, taps, shifted, finish)


def load_kernel(*refs):
    count = len(refs) // 2
    for copy in fetch(refs[:count], refs[count : 2 * count], refs[-1]):
        copy.wait()


def spectral_kernel(
    place, arrived, taps_in, forward, high_ref, low_ref, cos_ref, sin_ref, back_high, back_low,
    out, rows, sent, out_v, marks,
):
    rows[0:16, :] = jnp.zeros((16, L), F32)
    rows[16:, :] = arrived[...].astype(F32).reshape(16 * L, L)

    def array(a, c, back=0):
        return rows[pl.ds(16 * (1 - back) + 4 * a + c, L, stride=16), :]

    row_index = lax.broadcasted_iota(jnp.int32, (L, L), 0)
    lane_index = lax.broadcasted_iota(jnp.int32, (L, L), 1)
    chosen = (lax.broadcasted_iota(jnp.int32, (16, L), 1) == place[0]).astype(F32).astype(BF16)
    flip = (row_index + lane_index == L - 1).astype(F32).astype(BF16)
    onward = (lane_index == row_index + 1).astype(F32).astype(BF16)
    prods, earlier, gates, owns, others = [], [], [], [], []
    product_two = []
    for c in range(4):
        prods.append(array(1, c).astype(BF16))
        earlier.append(array(1, c, 1).astype(BF16))
        gates.append(array(2, c))
        taps = nt(chosen, taps_in[:, L * c : L * (c + 1)])[0:1, :]
        turned = pltpu.roll(jnp.broadcast_to(taps, (L, L)), 0, 1, stride=1, stride_axis=0)
        own = jnp.where(lane_index >= row_index, turned, 0.0).astype(BF16)
        other = jnp.where(lane_index < row_index, turned, 0.0).astype(BF16)
        owns.append(own)
        others.append(other)
        short_mix = nn(prods[c], own) + nn(earlier[c], other)
        product_two.append((gates[c] * short_mix).astype(BF16))

    cos_t, sin_t = cos_ref[...], sin_ref[...]
    high, low = high_ref[...], low_ref[...]

    def spectrum(columns):
        both = jnp.concatenate(columns, axis=1)
        first = nn(forward[...], jnp.concatenate([both, both], axis=0))
        turned = []
        for c in range(4):
            real = first[0:L, L * c : L * (c + 1)]
            imag = first[L : 2 * L, L * c : L * (c + 1)]
            turned.append(
                jnp.concatenate(
                    [real * cos_t + imag * sin_t, imag * cos_t - real * sin_t], axis=1
                )
            )
        coarse, fine = halves(jnp.concatenate(turned, axis=0))
        result = nn(coarse, high) + nn(coarse, low) + nn(fine, high)
        return result[:, 0:L], result[:, L : 2 * L]

    def restore(real, imag):
        coarse, fine = halves(jnp.concatenate([real, imag], axis=1))
        turned = nt(coarse, high) + nt(coarse, low) + nt(fine, high)
        columns = []
        for c in range(4):
            real = turned[L * c : L * (c + 1), 0:L]
            imag = turned[L * c : L * (c + 1), L : 2 * L]
            columns.append(
                jnp.concatenate(
                    [real * cos_t - imag * sin_t, imag * cos_t + real * sin_t], axis=0
                )
            )
        coarse, fine = halves(jnp.concatenate(columns, axis=1))
        return nn(back_high[...], coarse) + nn(back_high[...], fine) + nn(back_low[...], coarse)

    real_h, imag_h = spectrum([array(0, c).astype(BF16) for c in range(4)])
    real_g, imag_g = spectrum([array(3, c).astype(BF16) for c in range(4)])
    real_u, imag_u = spectrum(product_two)

    def store(a, c, value):
        sent[pl.ds(4 * a + c, L, stride=20), :] = value

    scaling = 1.0 / L
    back_two = restore(real_h * real_g + imag_h * imag_g, real_h * imag_g - imag_h * real_g)
    for c in range(4):
        part = slice(L * c, L * (c + 1))
        gated_one = (back_two[:, part] * gates[c]).astype(BF16)
        now = tn(nn(prods[c], flip).astype(BF16), gated_one)
        then = tn(nn(earlier[c], flip).astype(BF16), gated_one)
        pairs = jnp.where(lane_index >= L - 1 - row_index, now, then)
        turned = pltpu.roll(pairs, 1, 1, stride=1, stride_axis=0)
        filter_one = jnp.sum(turned, axis=0, keepdims=True) * scaling
        later = nn(onward, gated_one).astype(BF16)
        store(0, c, back_two[:, part])
        store(3, c, jnp.broadcast_to(filter_one, (L, L)))
        store(4, c, nt(gated_one, owns[c]) + nt(later, others[c]))
    long_mix = restore(real_h * real_u - imag_h * imag_u, real_h * imag_u + imag_h * real_u)
    for c in range(4):
        store(1, c, long_mix[:, L * c : L * (c + 1)])
    filter_two = restore(real_u * real_g + imag_u * imag_g, real_u * imag_g - imag_u * real_g)
    for c in range(4):
        store(2, c, filter_two[:, L * c : L * (c + 1)] * scaling)
    copies = []
    for k in range(4):
        part = pl.ds(5 * L * k, 5 * L)
        out_v[part, :] = sent[part, :].astype(BF16)
        copies.append(pltpu.make_async_copy(out_v.at[part, :], out.at[part, :], marks.at[k]))
        copies[k].start()
    for copy in copies:
        copy.wait()


def post_kernel(
    arrived, grad_two, short_mix, sq, lk, sk, sv, short_out, key_one_out, value_one_out, taps_out,
    query_out, key_out, filter_out, rows, results, marks,
):
    rows[...] = arrived[...].astype(F32)
    outs = (short_out, key_one_out, value_one_out, taps_out, query_out, key_out, filter_out)
    copies = []

    def array(a, c):
        return rows[pl.ds(4 * a + c, L, stride=20), :].T

    for c in range(4):
        lanes = slice(L * c, L * (c + 1))
        back_two, back_one = array(0, c), array(4, c)
        mix = short_mix[:, lanes]
        mixed = (sq[:, lanes].astype(F32) * mix).astype(BF16).astype(F32)
        mixed_grad = (back_two * lk[:, lanes].astype(F32)).astype(BF16).astype(F32)
        values = (
            mixed_grad * mix,
            back_one * sv[:, lanes].astype(F32),
            back_one * sk[:, lanes].astype(F32),
            array(3, c),
            grad_two[lanes, :].astype(F32).T * array(1, c),
            back_two * mixed,
            array(2, c),
        )
        for k, value in enumerate(values):
            results[k, :, lanes] = value.astype(BF16)
            copies.append(
                pltpu.make_async_copy(
                    results.at[k, :, lanes], outs[k].at[:, lanes], marks.at[k, c]
                )
            )
            copies[-1].start()
    for copy in copies:
        copy.wait()


def passed_along(block, axis, distance):
    devices = range(lax.axis_size(axis))
    route = [(i - distance, i) for i in devices if i - distance in devices]
    return lax.ppermute(block, axis, route)


def body(sq, sk, sv, taps, lq, lk, lf, weight, out_grad):
    block = jax.ShapeDtypeStruct((L, 4 * L), BF16)
    vmem = pl.BlockSpec(memory_space=pltpu.VMEM)
    smem = pl.BlockSpec(memory_space=pltpu.SMEM)
    hbm = pl.BlockSpec(memory_space=pltpu.HBM)
    tile = pltpu.VMEM((L, 4 * L), BF16)
    spread = pl.pallas_call(
        spread_kernel,
        out_shape=pltpu.HBM((4, L, 4 * L), BF16),
        in_specs=[hbm],
        out_specs=hbm,
        scratch_shapes=[tile, pltpu.SemaphoreType.DMA((2,)), pltpu.SemaphoreType.DMA((2, 4))],
        compiler_params=params(),
        name="spread",
    )(far(out_grad))
    grads = lax.all_to_all(spread, "tp", 0, 0, tiled=True)
    sent_shape = pltpu.HBM((L, 16, L), BF16)
    half = jax.ShapeDtypeStruct((L, 8, L), BF16)
    turned = jax.ShapeDtypeStruct((4 * L, L), BF16)
    staged, gate, prod, turned_lq, weight_v = pl.pallas_call(
        stage_kernel,
        out_shape=(sent_shape, half, block, turned, jax.ShapeDtypeStruct((4 * L, 16 * L), BF16)),
        in_specs=[hbm] * 7,
        out_specs=(hbm, vmem, vmem, vmem, vmem),
        scratch_shapes=[pltpu.VMEM((16 * L, L), F32), pltpu.VMEM((L, 16, L), BF16)]
        + [tile] * 6
        + [pltpu.SemaphoreType.DMA((8,))],
        compiler_params=params(),
        name="stage",
    )(*map(far, (lf, sk, sv, lk, sq, lq, weight)))
    before = passed_along(prod, CTX, 1)
    sent, grad_two = pl.pallas_call(
        join_kernel,
        out_shape=(sent_shape, turned),
        in_specs=[vmem, vmem, vmem, vmem, hbm],
        out_specs=(hbm, vmem),
        input_output_aliases={4: 0},
        scratch_shapes=[
            pltpu.VMEM((8 * L, L), F32), pltpu.VMEM((L, 8, L), BF16), pltpu.SemaphoreType.DMA,
        ],
        compiler_params=params(),
        name="join",
    )(grads, gate, weight_v, turned_lq, staged)
    arrived = lax.all_to_all(sent, CTX, 0, 0, tiled=True)
    constants = [jnp.asarray(t) for t in tables()]
    loaded = pl.pallas_call(
        load_kernel,
        out_shape=tuple(jax.ShapeDtypeStruct(t.shape, t.dtype) for t in constants),
        in_specs=[hbm] * 7,
        out_specs=(vmem,) * 7,
        scratch_shapes=[pltpu.SemaphoreType.DMA((7,))],
        compiler_params=params(),
        name="load",
    )(*map(far, constants))
    conv_scratch = [
        pltpu.VMEM((2 * L, 4 * L), F32), pltpu.VMEM((L, 4 * L), F32), pltpu.VMEM((2 * L, L), F32)
    ]
    short_mix = pl.pallas_call(
        mix_kernel,
        out_shape=jax.ShapeDtypeStruct((L, 4 * L), F32),
        scratch_shapes=conv_scratch,
        compiler_params=params(),
        name="mix",
    )(before, prod, taps)
    place = lax.axis_index(CTX).astype(jnp.int32).reshape(1)
    returned = pl.pallas_call(
        spectral_kernel,
        out_shape=pltpu.HBM((20 * L, L), BF16),
        in_specs=[smem] + [vmem] * 9,
        out_specs=hbm,
        scratch_shapes=[
            pltpu.VMEM((16 * L + 16, L), F32), pltpu.VMEM((20 * L, L), F32),
            pltpu.VMEM((20 * L, L), BF16), pltpu.SemaphoreType.DMA((4,)),
        ],
        compiler_params=params(),
        name="spectral",
    )(place, arrived, taps, *loaded)
    returned = returned.reshape(L, 5, 4, L)
    landed = lax.all_to_all(returned, CTX, 0, 0, tiled=True).reshape(20 * L, L)
    return pl.pallas_call(
        post_kernel,
        out_shape=(pltpu.HBM((L, 4 * L), BF16),) * 7,
        out_specs=(hbm,) * 7,
        scratch_shapes=[
            pltpu.VMEM((20 * L, L), F32), pltpu.VMEM((7, L, 4 * L), BF16),
            pltpu.SemaphoreType.DMA((7, 4)),
        ],
        compiler_params=params(),
        name="post",
    )(landed, grad_two, short_mix, sq, lk, sk, sv)


def solution(mesh):
    split = Mesh(
        mesh.devices.reshape(16, 4, 2, mesh.shape["tp"]), ("ctx_0", "ctx_1", "ctx_2", "tp")
    )
    rows = P(CTX, "tp")
    columns = P(None, "tp")
    return jax.shard_map(
        body,
        mesh=split,
        in_specs=(rows, rows, rows, columns, rows, rows, rows, P("tp", None), rows),
        out_specs=(rows, rows, rows, columns, rows, rows, rows),
        check_vma=False,
    )
```

```python
import jax
import jax.numpy as jnp
import numpy as np
from jax import lax
from jax.experimental import pallas as pl
from jax.experimental.pallas import tpu as pltpu
from jax.sharding import Mesh
from jax.sharding import PartitionSpec as P


CTX = ("ctx_0", "ctx_1", "ctx_2")
F32 = jnp.float32
BF16 = jnp.bfloat16
L = 128


def params():
    return pltpu.CompilerParams(vmem_limit_bytes=24 * 1024 * 1024)


def nn(a, b):
    return lax.dot_general(a, b, (((1,), (0,)), ((), ())), preferred_element_type=F32)


def nt(a, b):
    return lax.dot_general(a, b, (((1,), (1,)), ((), ())), preferred_element_type=F32)


def tn(a, b):
    return lax.dot_general(a, b, (((0,), (0,)), ((), ())), preferred_element_type=F32)


def halves(x):
    high = x.astype(BF16)
    return high, (x - high.astype(F32)).astype(BF16)


def np_halves(x):
    high = np.asarray(x, np.float32).astype(BF16)
    low = np.asarray(x - high.astype(np.float64), np.float32).astype(BF16)
    return high, low


def tables():
    whole = 2 * L * L
    k = np.arange(L) + 0.5
    n = np.arange(L)
    first = 2.0 * np.pi * np.outer(k, n) / (2 * L)
    one = np.concatenate([np.cos(first), -np.sin(first)], axis=0)
    one_high, one_low = np_halves(one)
    forward = np.concatenate([one_high, one_low], axis=1)
    back_high, back_low = np_halves(one.T * (2.0 / whole))
    twist = 2.0 * np.pi * np.outer(k, n) / whole
    cos_twist = np.cos(twist).astype(np.float32)
    sin_twist = np.sin(twist).astype(np.float32)
    second = 2.0 * np.pi * (np.outer(n, n) % L) / L
    cos_two, sin_two = np.cos(second), np.sin(second)
    two = np.block([[cos_two, -sin_two], [sin_two, cos_two]])
    two_high, two_low = np_halves(two)
    return (forward, two_high, two_low, cos_twist, sin_twist, back_high, back_low)


def far(array):
    return pltpu.with_memory_space_constraint(array, pltpu.HBM)


def fetch(sources, targets, marks):
    copies = [
        pltpu.make_async_copy(source, target, marks.at[k])
        for k, (source, target) in enumerate(zip(sources, targets))
    ]
    for copy in copies:
        copy.start()
    return copies


def put(rows, place, value):
    for c in range(4):
        rows[pl.ds(4 * place + c, L, stride=16), :] = value[:, L * c : L * (c + 1)].T


def spread_kernel(grads, out, grads_v, marks_in, marks_out):
    parts = [pl.ds(L // 2 * half, L // 2) for half in range(2)]
    copies = fetch(
        [grads.at[part, :] for part in parts], [grads_v.at[part, :] for part in parts], marks_in
    )
    outward = []
    for half, part in enumerate(parts):
        copies[half].wait()
        outward += fetch(
            [grads_v.at[part, :]] * 4, [out.at[k, part, :] for k in range(4)], marks_out.at[half]
        )
    for copy in outward:
        copy.wait()


def stage_kernel(
    lf, sk, sv, lk, sq, lq, weight, out, gate, prod, turned_lq, weight_v, rows, out_v, lf_v, sk_v,
    sv_v, lk_v, sq_v, lq_v, marks,
):
    copies = fetch(
        (lf, sk, sv, lk, sq, lq, weight), (lf_v, sk_v, sv_v, lk_v, sq_v, lq_v, weight_v), marks
    )
    put(rows, 3, jnp.zeros((L, 4 * L), F32))
    copies[0].wait()
    put(rows, 0, lf_v[...].astype(F32))
    copies[1].wait()
    copies[2].wait()
    product = (sk_v[...].astype(F32) * sv_v[...].astype(F32)).astype(BF16)
    prod[...] = product
    put(rows, 1, product.astype(F32))
    copies[3].wait()
    copies[4].wait()
    put(rows, 2, lk_v[...].astype(F32) * sq_v[...].astype(F32))
    out_v[...] = rows[...].reshape(L, 16, L).astype(BF16)
    gate[...] = out_v[:, 8:16, :]
    copy = pltpu.make_async_copy(out_v, out, marks.at[7])
    copy.start()
    copies[5].wait()
    turned_lq[...] = lq_v[...].astype(F32).T.astype(BF16)
    copies[6].wait()
    copy.wait()


def join_kernel(grads, gate, weight, turned_lq, staged, out, grad_two, rows, out_v, marks):
    rows[...] = gate[...].astype(F32).reshape(8 * L, L)
    total = nt(weight[:, 0:512], grads[0])
    for part in range(1, 4):
        total += nt(weight[:, 512 * part : 512 * (part + 1)], grads[part])
    grad_low = total.astype(BF16)
    gated = grad_low.astype(F32) * turned_lq[...].astype(F32)
    for c in range(4):
        rows[pl.ds(4 + c, L, stride=8), :] = gated[L * c : L * (c + 1), :]
    copies = []
    for k in range(4):
        part = slice(32 * k, 32 * (k + 1))
        out_v[part] = rows[256 * k : 256 * (k + 1), :].reshape(32, 8, L).astype(BF16)
        copies.append(pltpu.make_async_copy(out_v.at[part], out.at[part, 8:16, :], marks.at[k]))
        copies[k].start()
    grad_two[...] = grad_low
    for copy in copies:
        copy.wait()


def mix_loop(ext, taps, shifted, finish):
    def chunk(index, carry):
        lanes = pl.ds(pl.multiple_of(index * L, L), L)
        total = jnp.zeros((L, L), F32)
        for shift in range(8):
            shifted[8:256, :] = ext[8 - shift : 256 - shift, lanes]
            for group in range(16):
                start = L - 8 * group
                tap = 8 * group + shift
                total += taps[tap : tap + 1, lanes] * shifted[start : start + L, :]
        finish(lanes, total)
        return carry

    lax.fori_loop(0, 4, chunk, 0)


def mix_kernel(before, prod, taps_in, out, ext, taps, shifted):
    ext[0:L, :] = before[...].astype(F32)
    ext[L : 2 * L, :] = prod[...].astype(F32)
    taps[...] = taps_in[...].astype(F32)

    def finish(lanes, total):
        out[:, lanes] = total

    mix_loop(ext, taps, shifted, finish)


def load_kernel(*refs):
    count = len(refs) // 2
    for copy in fetch(refs[:count], refs[count : 2 * count], refs[-1]):
        copy.wait()


def spectral_kernel(
    place, arrived, taps_in, forward, high_ref, low_ref, cos_ref, sin_ref, back_high, back_low,
    out, rows, sent, out_v, marks,
):
    rows[0:16, :] = jnp.zeros((16, L), F32)
    rows[16:, :] = arrived[...].astype(F32).reshape(16 * L, L)

    def array(a, c, back=0):
        return rows[pl.ds(16 * (1 - back) + 4 * a + c, L, stride=16), :]

    row_index = lax.broadcasted_iota(jnp.int32, (L, L), 0)
    lane_index = lax.broadcasted_iota(jnp.int32, (L, L), 1)
    chosen = (lax.broadcasted_iota(jnp.int32, (16, L), 1) == place[0]).astype(F32).astype(BF16)
    flip = (row_index + lane_index == L - 1).astype(F32).astype(BF16)
    onward = (lane_index == row_index + 1).astype(F32).astype(BF16)
    prods, earlier, gates, owns, others = [], [], [], [], []
    product_two = []
    for c in range(4):
        prods.append(array(1, c).astype(BF16))
        earlier.append(array(1, c, 1).astype(BF16))
        gates.append(array(2, c))
        taps = nt(chosen, taps_in[:, L * c : L * (c + 1)])[0:1, :]
        turned = pltpu.roll(jnp.broadcast_to(taps, (L, L)), 0, 1, stride=1, stride_axis=0)
        own = jnp.where(lane_index >= row_index, turned, 0.0).astype(BF16)
        other = jnp.where(lane_index < row_index, turned, 0.0).astype(BF16)
        owns.append(own)
        others.append(other)
        short_mix = nn(prods[c], own) + nn(earlier[c], other)
        product_two.append((gates[c] * short_mix).astype(BF16))

    cos_t, sin_t = cos_ref[...], sin_ref[...]
    high, low = high_ref[...], low_ref[...]

    def spectrum(columns):
        both = jnp.concatenate(columns, axis=1)
        first = nn(forward[...], jnp.concatenate([both, both], axis=0))
        turned = []
        for c in range(4):
            real = first[0:L, L * c : L * (c + 1)]
            imag = first[L : 2 * L, L * c : L * (c + 1)]
            turned.append(
                jnp.concatenate(
                    [real * cos_t + imag * sin_t, imag * cos_t - real * sin_t], axis=1
                )
            )
        coarse, fine = halves(jnp.concatenate(turned, axis=0))
        result = nn(coarse, high) + nn(coarse, low) + nn(fine, high)
        return result[:, 0:L], result[:, L : 2 * L]

    def restore(real, imag):
        coarse, fine = halves(jnp.concatenate([real, imag], axis=1))
        turned = nt(coarse, high) + nt(coarse, low) + nt(fine, high)
        columns = []
        for c in range(4):
            real = turned[L * c : L * (c + 1), 0:L]
            imag = turned[L * c : L * (c + 1), L : 2 * L]
            columns.append(
                jnp.concatenate(
                    [real * cos_t - imag * sin_t, imag * cos_t + real * sin_t], axis=0
                )
            )
        coarse, fine = halves(jnp.concatenate(columns, axis=1))
        return nn(back_high[...], coarse) + nn(back_high[...], fine) + nn(back_low[...], coarse)

    real_h, imag_h = spectrum([array(0, c).astype(BF16) for c in range(4)])
    real_g, imag_g = spectrum([array(3, c).astype(BF16) for c in range(4)])
    real_u, imag_u = spectrum(product_two)

    def store(a, c, value):
        sent[pl.ds(4 * a + c, L, stride=20), :] = value

    scaling = 1.0 / L
    back_two = restore(real_h * real_g + imag_h * imag_g, real_h * imag_g - imag_h * real_g)
    for c in range(4):
        part = slice(L * c, L * (c + 1))
        gated_one = (back_two[:, part] * gates[c]).astype(BF16)
        now = tn(nn(prods[c], flip).astype(BF16), gated_one)
        then = tn(nn(earlier[c], flip).astype(BF16), gated_one)
        pairs = jnp.where(lane_index >= L - 1 - row_index, now, then)
        turned = pltpu.roll(pairs, 1, 1, stride=1, stride_axis=0)
        filter_one = jnp.sum(turned, axis=0, keepdims=True) * scaling
        later = nn(onward, gated_one).astype(BF16)
        store(0, c, back_two[:, part])
        store(3, c, jnp.broadcast_to(filter_one, (L, L)))
        store(4, c, nt(gated_one, owns[c]) + nt(later, others[c]))
    long_mix = restore(real_h * real_u - imag_h * imag_u, real_h * imag_u + imag_h * real_u)
    for c in range(4):
        store(1, c, long_mix[:, L * c : L * (c + 1)])
    filter_two = restore(real_u * real_g + imag_u * imag_g, real_u * imag_g - imag_u * real_g)
    for c in range(4):
        store(2, c, filter_two[:, L * c : L * (c + 1)] * scaling)
    copies = []
    for k in range(4):
        part = pl.ds(5 * L * k, 5 * L)
        out_v[part, :] = sent[part, :].astype(BF16)
        copies.append(pltpu.make_async_copy(out_v.at[part, :], out.at[part, :], marks.at[k]))
        copies[k].start()
    for copy in copies:
        copy.wait()


def post_kernel(
    arrived, grad_two, short_mix, sq, lk, sk, sv, short_out, key_one_out, value_one_out, taps_out,
    query_out, key_out, filter_out, rows, results, marks,
):
    rows[...] = arrived[...].astype(F32)
    outs = (short_out, key_one_out, value_one_out, taps_out, query_out, key_out, filter_out)
    copies = []

    def array(a, c):
        return rows[pl.ds(4 * a + c, L, stride=20), :].T

    for c in range(4):
        lanes = slice(L * c, L * (c + 1))
        back_two, back_one = array(0, c), array(4, c)
        mix = short_mix[:, lanes]
        mixed = (sq[:, lanes].astype(F32) * mix).astype(BF16).astype(F32)
        mixed_grad = (back_two * lk[:, lanes].astype(F32)).astype(BF16).astype(F32)
        values = (
            mixed_grad * mix,
            back_one * sv[:, lanes].astype(F32),
            back_one * sk[:, lanes].astype(F32),
            array(3, c),
            grad_two[lanes, :].astype(F32).T * array(1, c),
            back_two * mixed,
            array(2, c),
        )
        for k, value in enumerate(values):
            results[k, :, lanes] = value.astype(BF16)
            copies.append(
                pltpu.make_async_copy(
                    results.at[k, :, lanes], outs[k].at[:, lanes], marks.at[k, c]
                )
            )
            copies[-1].start()
    for copy in copies:
        copy.wait()


def passed_along(block, axis, distance):
    devices = range(lax.axis_size(axis))
    route = [(i - distance, i) for i in devices if i - distance in devices]
    return lax.ppermute(block, axis, route)


def body(sq, sk, sv, taps, lq, lk, lf, weight, out_grad):
    block = jax.ShapeDtypeStruct((L, 4 * L), BF16)
    vmem = pl.BlockSpec(memory_space=pltpu.VMEM)
    smem = pl.BlockSpec(memory_space=pltpu.SMEM)
    hbm = pl.BlockSpec(memory_space=pltpu.HBM)
    tile = pltpu.VMEM((L, 4 * L), BF16)
    spread = pl.pallas_call(
        spread_kernel,
        out_shape=pltpu.HBM((4, L, 4 * L), BF16),
        in_specs=[hbm],
        out_specs=hbm,
        scratch_shapes=[tile, pltpu.SemaphoreType.DMA((2,)), pltpu.SemaphoreType.DMA((2, 4))],
        compiler_params=params(),
        name="spread",
    )(far(out_grad))
    grads = lax.all_to_all(spread, "tp", 0, 0, tiled=True)
    sent_shape = pltpu.HBM((L, 16, L), BF16)
    half = jax.ShapeDtypeStruct((L, 8, L), BF16)
    turned = jax.ShapeDtypeStruct((4 * L, L), BF16)
    staged, gate, prod, turned_lq, weight_v = pl.pallas_call(
        stage_kernel,
        out_shape=(sent_shape, half, block, turned, jax.ShapeDtypeStruct((4 * L, 16 * L), BF16)),
        in_specs=[hbm] * 7,
        out_specs=(hbm, vmem, vmem, vmem, vmem),
        scratch_shapes=[pltpu.VMEM((16 * L, L), F32), pltpu.VMEM((L, 16, L), BF16)]
        + [tile] * 6
        + [pltpu.SemaphoreType.DMA((8,))],
        compiler_params=params(),
        name="stage",
    )(*map(far, (lf, sk, sv, lk, sq, lq, weight)))
    before = passed_along(prod, CTX, 1)
    sent, grad_two = pl.pallas_call(
        join_kernel,
        out_shape=(sent_shape, turned),
        in_specs=[vmem, vmem, vmem, vmem, hbm],
        out_specs=(hbm, vmem),
        input_output_aliases={4: 0},
        scratch_shapes=[
            pltpu.VMEM((8 * L, L), F32), pltpu.VMEM((L, 8, L), BF16), pltpu.SemaphoreType.DMA((4,)),
        ],
        compiler_params=params(),
        name="join",
    )(grads, gate, weight_v, turned_lq, staged)
    arrived = lax.all_to_all(sent, CTX, 0, 0, tiled=True)
    constants = [jnp.asarray(t) for t in tables()]
    loaded = pl.pallas_call(
        load_kernel,
        out_shape=tuple(jax.ShapeDtypeStruct(t.shape, t.dtype) for t in constants),
        in_specs=[hbm] * 7,
        out_specs=(vmem,) * 7,
        scratch_shapes=[pltpu.SemaphoreType.DMA((7,))],
        compiler_params=params(),
        name="load",
    )(*map(far, constants))
    conv_scratch = [
        pltpu.VMEM((2 * L, 4 * L), F32), pltpu.VMEM((L, 4 * L), F32), pltpu.VMEM((2 * L, L), F32)
    ]
    short_mix = pl.pallas_call(
        mix_kernel,
        out_shape=jax.ShapeDtypeStruct((L, 4 * L), F32),
        scratch_shapes=conv_scratch,
        compiler_params=params(),
        name="mix",
    )(before, prod, taps)
    place = lax.axis_index(CTX).astype(jnp.int32).reshape(1)
    returned = pl.pallas_call(
        spectral_kernel,
        out_shape=pltpu.HBM((20 * L, L), BF16),
        in_specs=[smem] + [vmem] * 9,
        out_specs=hbm,
        scratch_shapes=[
            pltpu.VMEM((16 * L + 16, L), F32), pltpu.VMEM((20 * L, L), F32),
            pltpu.VMEM((20 * L, L), BF16), pltpu.SemaphoreType.DMA((4,)),
        ],
        compiler_params=params(),
        name="spectral",
    )(place, arrived, taps, *loaded)
    returned = returned.reshape(L, 5, 4, L)
    landed = lax.all_to_all(returned, CTX, 0, 0, tiled=True).reshape(20 * L, L)
    return pl.pallas_call(
        post_kernel,
        out_shape=(pltpu.HBM((L, 4 * L), BF16),) * 7,
        out_specs=(hbm,) * 7,
        scratch_shapes=[
            pltpu.VMEM((20 * L, L), F32), pltpu.VMEM((7, L, 4 * L), BF16),
            pltpu.SemaphoreType.DMA((7, 4)),
        ],
        compiler_params=params(),
        name="post",
    )(landed, grad_two, short_mix, sq, lk, sk, sv)


def solution(mesh):
    split = Mesh(
        mesh.devices.reshape(16, 4, 2, mesh.shape["tp"]), ("ctx_0", "ctx_1", "ctx_2", "tp")
    )
    rows = P(CTX, "tp")
    columns = P(None, "tp")
    return jax.shard_map(
        body,
        mesh=split,
        in_specs=(rows, rows, rows, columns, rows, rows, rows, P("tp", None), rows),
        out_specs=(rows, rows, rows, columns, rows, rows, rows),
        check_vma=False,
    )
```
